256 devices in a mesh: seg: 64 (over x, z, core), pitch: 4 (over y).
Axes of the slice: x: 4, y: 4, z: 8, core: 2. Of those that a mesh axis runs over, the one named last changes fastest.
Arguments:
- state: float32 [1024, 8, 5, 49, 128], P('seg', 'pitch'), may hold values from -6 to 6
- advect: float32 [1024, 8, 5, 128], P('seg', 'pitch'), may hold values from 0.2 to 1
- viscous: float32 [1024, 8, 5, 128], P('seg', 'pitch'), may hold values from 0.1 to 0.5
- inverse: bfloat16 [1024, 8, 5, 5, 128], P('seg', 'pitch'), as said below
- lower: float32 [1024, 8, 5, 5, 128], P('seg', 'pitch'), as said below
- upper: float32 [1024, 8, 5, 5, 128], P('seg', 'pitch'), as said below
- blades: int32 [2], replicated, may hold values from 20 to 90
- harmonic: int32 [24], replicated, may hold values from 1 to 8, as said below
Outputs:
- update: float32 [1024, 8, 5, 49, 128], P('seg', 'pitch')
The draws below stay inside these ranges and needn't reach their ends.
Inputs may be any that keep to these rules, and one draw needn't show every extreme that they name: inverse holds each cell's given block inverse. lower holds each cell's upstream coupling, already multiplied by the block inverse and negated. upper holds each cell's downstream coupling, already multiplied by the block inverse and negated. `harmonic`: the mode multiples are not all equal.
All inputs are finite; a program needn't handle non-finite values.
Results may differ from the reference program's by a relative error of at most 0.0003.
Values sent between devices are 32-bit elements; how exact they have to be, the bound alone decides.
A program may use at most 128 MiB of HBM per device.

```python
import math
import jax
import jax.numpy as jnp
from jax import lax

SPANWISE_NODES = 128
HARM = 24
NT = 49
STREAMWISE_NODES = 1024
BLADEWISE_NODES = 8


def product_block(left, right):
    return jnp.sum(left[..., :, :, None, :] * right[..., None, :, :, :], axis=-3)


def unit_inverse(nilpotent, identity):
    series_term = identity
    total = identity
    for order_id in range(4):
        series_term = product_block(series_term, -nilpotent)
        total = total + series_term
    return total


def coupling(key, orientation):
    stochastic_seeds = jax.random.split(key, 9)
    spread = 0.35
    slow_share = 0.5
    index_ids = jnp.arange(5)
    strict_low = (index_ids[:, None] > index_ids[None, :]).astype(jnp.float32)[None, :, :, None]
    strict_high = (index_ids[:, None] < index_ids[None, :]).astype(jnp.float32)[None, :, :, None]
    lower_mix = jax.random.uniform(stochastic_seeds[0], (BLADEWISE_NODES, 5, 5, SPANWISE_NODES), minval=-spread, maxval=spread) * strict_low
    upper_mix = jax.random.uniform(stochastic_seeds[7], (BLADEWISE_NODES, 5, 5, SPANWISE_NODES), minval=-spread, maxval=spread) * strict_high
    identity = jnp.eye(5, dtype=jnp.float32)[None, :, :, None] * jnp.ones((BLADEWISE_NODES, 1, 1, SPANWISE_NODES), jnp.float32)
    eigen_basis = product_block(identity + lower_mix, identity + upper_mix)
    inverse_basis = product_block(unit_inverse(upper_mix, identity), unit_inverse(lower_mix, identity))
    slow_mask = jax.random.uniform(stochastic_seeds[1], (BLADEWISE_NODES, 5, SPANWISE_NODES)) < slow_share
    slow_rate = math.log(10.0) * jax.random.uniform(stochastic_seeds[2], (BLADEWISE_NODES, 5, SPANWISE_NODES), minval=0.1, maxval=0.4) / STREAMWISE_NODES
    lengths = jnp.exp(jax.random.uniform(stochastic_seeds[3], (BLADEWISE_NODES, 5, SPANWISE_NODES), minval=math.log(4.0), maxval=math.log(30.0)))
    decay_rate = jnp.where(slow_mask, slow_rate, 1.0 / lengths)
    jitter = jax.random.uniform(stochastic_seeds[4], (STREAMWISE_NODES, BLADEWISE_NODES, 5, SPANWISE_NODES), minval=0.5, maxval=1.5)
    damping_multipliers = jnp.exp(-decay_rate[None] * jitter)
    spike_node_total = jax.random.randint(stochastic_seeds[5], (2, BLADEWISE_NODES, SPANWISE_NODES), 0, STREAMWISE_NODES)
    node_locations = jnp.arange(STREAMWISE_NODES)[:, None, None]
    spike_threshold = jax.random.uniform(stochastic_seeds[6], (2, BLADEWISE_NODES, 5, SPANWISE_NODES), minval=0.55, maxval=0.8)
    primary_strike = (node_locations == spike_node_total[0][None])[:, :, None, :]
    secondary_strike = (node_locations == spike_node_total[1][None])[:, :, None, :]
    damping_multipliers = damping_multipliers * jnp.where(primary_strike, spike_threshold[0][None], 1.0) * jnp.where(secondary_strike, spike_threshold[1][None], 1.0)
    unit = jnp.eye(5, dtype=jnp.float32)[None, None, :, :, None]
    mixing_field = jax.random.uniform(stochastic_seeds[8], (STREAMWISE_NODES, BLADEWISE_NODES, 5, 5, SPANWISE_NODES), minval=-1.0, maxval=1.0) * (1.0 - unit)
    inner_block = unit * damping_multipliers[:, :, :, None, :] + 0.2 * (1.0 - damping_multipliers)[:, :, :, None, :] * mixing_field
    inner_block = orientation * inner_block
    return jnp.einsum('pabr,zpbcr,pcdr->zpadr', eigen_basis, inner_block, inverse_basis).astype(jnp.float32)


def draw_lower(key, part):
    return coupling(jax.random.fold_in(key, 11), 1.0)


def draw_upper(key, part):
    return coupling(jax.random.fold_in(key, 23), -1.0)


def draw_harmonic(key, part):
    multiples = jax.random.randint(jax.random.fold_in(key, 53), (HARM,), 1, 9)
    second_value = 1 + jnp.mod(multiples[0], 8)
    position = jnp.arange(HARM)
    return jnp.where(position == 1, second_value, multiples).astype(jnp.int32)


def draw_inverse(key, part):
    stochastic_seeds = jax.random.split(jax.random.fold_in(key, 37), 2)
    diagonal = jnp.exp(jax.random.uniform(stochastic_seeds[0], (STREAMWISE_NODES, BLADEWISE_NODES, 5, SPANWISE_NODES), minval=math.log(0.5), maxval=math.log(2.0)))
    offdiag = jax.random.uniform(stochastic_seeds[1], (STREAMWISE_NODES, BLADEWISE_NODES, 5, 5, SPANWISE_NODES), minval=-0.3, maxval=0.3)
    unit = jnp.eye(5, dtype=jnp.float32)[None, None, :, :, None]
    whole = unit * diagonal[:, :, :, None, :] + (1.0 - unit) * offdiag
    scaling = 1.0 / math.sqrt(STREAMWISE_NODES)
    return (whole * scaling).astype(jnp.bfloat16)


def block_scale(own_key, extent, cuts, least, high):
    loudness, own = 1.0, jax.random.fold_in(own_key, 6)
    for dim, shards_of in cuts:
        steps = jnp.exp(jax.random.uniform(jax.random.fold_in(own, dim), (shards_of,), jnp.float32, least / len(cuts), high / len(cuts)))
        loudness = loudness * jnp.repeat(steps, extent[dim] // shards_of).reshape([-1 if axis == dim else 1 for axis in range(len(extent))])
    return loudness


def centred(stream_key, shape, scale, bound, cuts=(), kind=jnp.bfloat16):
    drawn = jax.random.normal(stream_key, shape, jnp.float32) * scale
    if len(cuts) > 0:
        drawn = block_scale(stream_key, shape, cuts, -0.22, 0.18) * drawn
    return jnp.clip(drawn, min=-bound, max=bound).astype(kind)


def setup_inputs(seed: int = 0) -> dict:
    key_list = jax.random.split(jax.random.key(seed), 9)
    return {
        "state": centred(key_list[0], (STREAMWISE_NODES, BLADEWISE_NODES, 5, NT, SPANWISE_NODES), 1.0, 6.0, ((0, 64), (1, 4)), jnp.float32),
        "advect": jnp.clip(jnp.exp(math.log(1.0) - 1.609438 * jax.random.uniform(key_list[1], (STREAMWISE_NODES, BLADEWISE_NODES, 5, SPANWISE_NODES), jnp.float32) ** block_scale(key_list[1], (STREAMWISE_NODES, BLADEWISE_NODES, 5, SPANWISE_NODES), ((0, 64), (1, 4)), -0.2, 0.2)), 0.2, 1.0),
        "viscous": jnp.clip(jnp.exp(math.log(0.5) - 1.609438 * jax.random.uniform(key_list[2], (STREAMWISE_NODES, BLADEWISE_NODES, 5, SPANWISE_NODES), jnp.float32) ** block_scale(key_list[2], (STREAMWISE_NODES, BLADEWISE_NODES, 5, SPANWISE_NODES), ((0, 64), (1, 4)), -0.2, 0.2)), 0.1, 0.5),
        "inverse": draw_inverse(jax.random.fold_in(key_list[8], 71), 0),
        "lower": draw_lower(jax.random.fold_in(key_list[8], 71), 0),
        "upper": draw_upper(jax.random.fold_in(key_list[8], 71), 0),
        "blades": jax.random.randint(key_list[6], (2,), 20, 91).astype(jnp.int32),
        "harmonic": draw_harmonic(jax.random.fold_in(key_list[8], 71), 0),
    }


def spectral_tables(blades, harmonic, fourier_components):
    sampled_moments = 2 * fourier_components + 1
    moment_number = jnp.arange(sampled_moments, dtype=jnp.int32)
    blade_spacing_displacement = moment_number[:, None] - moment_number[None, :]
    cyclic_folded = jnp.mod(blade_spacing_displacement, sampled_moments)
    parity = 1.0 - 2.0 * jnp.mod(blade_spacing_displacement, 2).astype(jnp.float32)
    protected_sinus = jnp.where(blade_spacing_displacement == 0, jnp.float32(1.0), jnp.sin(math.pi * blade_spacing_displacement.astype(jnp.float32) / sampled_moments))
    derive = jnp.where(blade_spacing_displacement == 0, jnp.float32(0.0), 0.5 * parity / protected_sinus)
    rotor_blades = blades[0].astype(jnp.float32)
    stator = blades[1].astype(jnp.float32)
    blade_ratio = stator / rotor_blades
    frequency = blade_ratio / fourier_components
    fourier_wavenumbers = jnp.arange(1, fourier_components + 1, dtype=jnp.int32)
    lag_amounts = 2.0 * math.pi * harmonic.astype(jnp.float32) * blade_ratio
    lag_radians = jnp.mod(fourier_wavenumbers[:, None, None] * cyclic_folded[None], sampled_moments).astype(jnp.float32) * (2.0 * math.pi / sampled_moments)
    forward_lag_angle = (1.0 + 2.0 * jnp.sum(jnp.cos(lag_radians + lag_amounts[:, None, None]), axis=0)) / sampled_moments
    rearward_displacement = (1.0 + 2.0 * jnp.sum(jnp.cos(lag_radians - lag_amounts[:, None, None]), axis=0)) / sampled_moments
    return derive, frequency, forward_lag_angle, rearward_displacement


def apply_block(left, right):
    return jnp.sum(left[..., :, :, None, :] * right[..., None, :, :, :], axis=-3)


def reference(state, advect, viscous, inverse, lower, upper, blades, harmonic):
    fourier_components = harmonic.shape[0]
    derive, frequency, forward_lag_angle, rearward_displacement = spectral_tables(blades, harmonic, fourier_components)
    exact = lax.Precision.HIGHEST
    ghost_low = jnp.einsum('nm,zvmr->zvnr', rearward_displacement, state[:, -1], precision=exact)
    ghost_high = jnp.einsum('nm,zvmr->zvnr', forward_lag_angle, state[:, 0], precision=exact)
    lowside = jnp.concatenate([ghost_low[:, None], state[:, :-1]], axis=1)
    highside = jnp.concatenate([state[:, 1:], ghost_high[:, None]], axis=1)
    zeros_rim = jnp.zeros_like(state[:1])
    upstream = jnp.concatenate([zeros_rim, state[:-1]], axis=0)
    downstream = jnp.concatenate([state[1:], zeros_rim], axis=0)
    axial_term = advect[:, :, :, None, :] * (upstream - downstream)
    pitch_term = viscous[:, :, :, None, :] * (lowside + highside - 2.0 * state)
    timing = frequency * jnp.einsum('nm,zpvmr->zpvnr', derive, state, precision=exact)
    residual = axial_term + pitch_term - timing

    def forward(current, pieces):
        inverse_cell, source_cell, coupling_cell = pieces
        current = apply_block(inverse_cell.astype(jnp.float32), source_cell) + apply_block(coupling_cell, current)
        return current, current

    initial = jnp.zeros_like(state[0])
    _, sweep_rows = lax.scan(forward, initial, (inverse, residual, lower))

    def backward(current, pieces):
        solved, coupling_cell = pieces
        current = solved + apply_block(coupling_cell, current)
        return current, current

    _, update = lax.scan(backward, initial, (sweep_rows, upper), reverse=True)
    return update
```

```python
import functools
import math

import jax
import jax.numpy as jnp
import numpy as np
from jax import lax
from jax.experimental import pallas as pl
from jax.experimental.pallas import tpu as pltpu
from jax.sharding import PartitionSpec as P

MESH = pl.DeviceIdType.MESH
ANY = pl.BlockSpec(memory_space=pl.ANY)
V = 5
R = 128
PACK = 64
F32 = jnp.float32


def tables(nt):
    harm = (nt - 1) // 2
    n = np.arange(nt)
    diff = n[:, None] - n[None, :]
    derive = np.where(diff == 0, 0.0, 0.5 * (1 - 2 * (diff % 2)) / np.where(diff == 0, 1.0, np.sin(np.pi * diff / nt)))
    angle = 2 * np.pi * ((n[:, None] * np.arange(1, harm + 1)[None, :]) % nt) / nt
    cosine, sine = np.cos(angle), np.sin(angle)
    rows = 56
    x = np.zeros((rows, R))
    y = np.zeros((rows, R))
    x[:nt, 0] = 1.0 / nt
    x[:nt, 1 : harm + 1], x[:nt, harm + 1 : nt] = 2 * cosine / nt, 2 * sine / nt
    y[:nt, 1 : harm + 1], y[:nt, harm + 1 : nt] = -2 * sine / nt, 2 * cosine / nt
    right = np.zeros((R, 2 * R))
    wide = np.zeros((rows, 2 * R))
    for third in range(3):
        at = slice(third * PACK, third * PACK + nt)
        right[0, at] = 1.0
        right[1 : harm + 1, at], right[harm + 1 : nt, at] = cosine.T, sine.T
        wide[:nt, at] = derive
    return tuple(np.asarray(a, np.float32) for a in (x, y, right, wide))


def bc(tile, k):
    return jnp.broadcast_to(tile[k : k + 1, :], (8, R))


def total(terms):
    terms = list(terms)
    while len(terms) > 1:
        terms = [a + b for a, b in zip(terms[::2], terms[1::2])] + ([terms[-1]] if len(terms) % 2 else [])
    return terms[0]


def matvec(row, vec):
    return [total([row(a, k) * vec[k] for k in range(V)]) for a in range(V)]


def colvec(cols, vec):
    return total([cols[k] * bc(vec, k) for k in range(V)])


def colmat(cols, mat):
    return [colvec(cols, m) for m in mat]


def plus(a, b):
    return [x + y for x, y in zip(a, b)]


def kernel(
    nx, nz, ny, cells, nt,
    state, advect, viscous, inverse, lower, upper, row, ex, ey, eright, ewide,
    out,
    st, pit, ghost, work, adv, vis, inv16, inv, low, upp, rowv, exv, eyv, erv, ewv, wder, wghost,
    pres, qres, mloc, cmat, zmat, resp, xmat,
    csend, cbuf, zsend, zbuf, sol, xbuf, sx, ysend, ybuf, fsend, infl,
    ld, axs, axr, pits, pitr, mcs, mcr, mzs, mzr, mxs, mxr,
    cs, cr, zs, zr, xs, xr, ys, yr, fs, fr, outs,
):
    tiles = (nt + 7) // 8
    last = nt - 8 * (tiles - 1)
    seg = lax.axis_index("seg")
    y = lax.axis_index("pitch")
    core = lax.rem(seg, 2)
    z = lax.rem(seg // 2, nz)
    x = seg // (2 * nz)
    nseg = 2 * nx * nz
    mate = seg + 1 - 2 * core
    yup, ydn = lax.rem(y + 1, ny), lax.rem(y + ny - 1, ny)

    def zpeer(i):
        zz = lax.rem(z + i, nz)
        return zz, (x * nz + zz) * 2 + core

    def xpeer(i):
        xx = lax.rem(x + i, nx)
        return xx, (xx * nz + z) * 2 + core

    def remote(src, dst, send, recv, **to):
        return pltpu.make_async_remote_copy(
            src_ref=src, dst_ref=dst, send_sem=send, recv_sem=recv, device_id=to, device_id_type=MESH
        )

    @pl.loop(0, cells + 2)
    def _(c):
        for p in range(2):
            for v in range(V):
                st[c, p, v, pl.ds(nt, 8 * tiles - nt), :] = jnp.zeros((8 * tiles - nt, R), F32)

    loads = [
        pltpu.make_async_copy(row, rowv, ld.at[0]),
        pltpu.make_async_copy(ex, exv, ld.at[1]),
        pltpu.make_async_copy(ey, eyv, ld.at[2]),
        pltpu.make_async_copy(eright, erv, ld.at[3]),
        pltpu.make_async_copy(ewide, ewv, ld.at[4]),
        pltpu.make_async_copy(state, st.at[pl.ds(1, cells), :, :, pl.ds(0, nt), :], ld.at[5]),
        pltpu.make_async_copy(lower, low, ld.at[6]),
        pltpu.make_async_copy(upper, upp, ld.at[7]),
        pltpu.make_async_copy(advect, adv, ld.at[8]),
        pltpu.make_async_copy(viscous, vis, ld.at[9]),
        pltpu.make_async_copy(inverse, inv16, ld.at[10]),
    ]
    for c in loads:
        c.start()

    barrier = pltpu.get_barrier_semaphore()

    def greet(**to):
        pl.semaphore_signal(barrier, inc=1, device_id=to, device_id_type=MESH)

    greet(pitch=yup)
    greet(pitch=ydn)
    greet(seg=mate)
    greet(seg=lax.rem(seg + 1, nseg))
    greet(seg=lax.rem(seg + nseg - 1, nseg))

    @pl.loop(1, nz)
    def _(i):
        greet(seg=zpeer(i)[1])

    @pl.loop(1, nx)
    def _(i):
        greet(seg=xpeer(i)[1])

    pl.semaphore_wait(barrier, 5 + nz - 1 + nx - 1)

    def rows_of(k):
        return pl.ds(8 * (tiles - 1), last) if k == 0 else pl.ds(8 * (k - 1), 8)

    def pitch_copy(k, d, raw, cellrange=None):
        at = rows_of(k)
        zr_ = pl.ds(0, cells) if cellrange is None else cellrange
        src = state.at[zr_, 1 - d, :, at, :] if raw else ghost.at[zr_, :, at, :]
        return remote(
            src, pit.at[d, zr_, :, at, :], pits.at[d, k], pitr.at[d, k], pitch=yup if d == 0 else ydn
        )

    for d in range(2):
        wraps = (y == ny - 1) if d == 0 else (y == 0)

        @pl.when(jnp.logical_not(wraps))
        def _():
            for k in range(tiles):
                pitch_copy(k, d, True).start()

    ax_up = remote(state.at[cells - 1], st.at[0, :, :, pl.ds(0, nt), :], axs.at[0], axr.at[0], seg=lax.rem(seg + 1, nseg))
    ax_dn = remote(
        state.at[0], st.at[cells + 1, :, :, pl.ds(0, nt), :], axs.at[1], axr.at[1], seg=lax.rem(seg + nseg - 1, nseg)
    )

    @pl.when(seg < nseg - 1)
    def _():
        ax_up.start()

    @pl.when(seg > 0)
    def _():
        ax_dn.start()

    for edge, cell in ((seg == 0, 0), (seg == nseg - 1, cells + 1)):

        @pl.when(edge)
        def _():
            for p in range(2):
                for v in range(V):
                    st[cell, p, v, pl.ds(0, nt), :] = jnp.zeros((nt, R), F32)

    def split3(wide):
        high = wide.astype(jnp.bfloat16)
        low_ = (wide - high.astype(F32)).astype(jnp.bfloat16)
        lane = lax.broadcasted_iota(jnp.int32, wide.shape, 1)
        return jnp.where(lane < 2 * PACK, high.astype(F32), low_.astype(F32)).astype(jnp.bfloat16)[:, : 3 * PACK]

    def stacked(cell):
        s = jnp.concatenate([cell, jnp.zeros((PACK - 8 * tiles, R), F32)], 0)
        high = s.astype(jnp.bfloat16)
        low_ = (s - high.astype(F32)).astype(jnp.bfloat16)
        return jnp.concatenate([high, low_, high], 0)

    def pair(weights, c, p, v):
        rhs = jnp.concatenate([stacked(st[1 + c, p, v]), stacked(st[2 + c, p, v])], 1)
        both = jnp.dot(weights[...], rhs, preferred_element_type=F32)
        return both[:, :R], both[:, R:]

    for c in loads[:6]:
        c.wait()

    @pl.when((y == 0) | (y == ny - 1))
    def _():
        sign = jnp.where(y == 0, 1.0, -1.0).astype(F32)
        e = exv[...] * rowv[pl.ds(0, 1), :] + eyv[...] * (rowv[pl.ds(1, 1), :] * sign)
        wghost[...] = split3(jnp.dot(e, erv[...], precision=lax.Precision.HIGHEST, preferred_element_type=F32))
        p = jnp.where(y == 0, 0, 1)

        @pl.loop(0, cells // 2)
        def _(h):
            for v in range(V):
                a, b = pair(wghost, 2 * h, p, v)
                ghost[2 * h, v] = a
                ghost[2 * h + 1, v] = b
            for d in range(2):

                @pl.when((y == ny - 1) if d == 0 else (y == 0))
                def _():
                    for k in range(2):
                        pitch_copy(k, d, False, pl.ds(2 * h, 2)).start()

        for d in range(2):

            @pl.when((y == ny - 1) if d == 0 else (y == 0))
            def _():
                for k in range(2, tiles):
                    pitch_copy(k, d, False).start()

    for c in loads[6:]:
        c.wait()

    sub = lax.broadcasted_iota(jnp.int32, (8, R), 0)
    unit = [jnp.where(sub == v, 1.0, 0.0).astype(F32) for v in range(V)]
    zero = jnp.zeros((8, R), F32)

    def rowsof(ref, c, p):
        return lambda a, k: ref[c, p, a, pl.ds(k, 1), :]

    def forward_h(c, carry):
        new = []
        for p in range(2):
            h = matvec(rowsof(low, c, p), carry[p])
            for a in range(V):
                pres[c, p, a] = h[a]
            new.append(h)
        return new

    tail = lax.fori_loop(0, cells, forward_h, [list(unit), list(unit)])
    for p in range(2):
        for a in range(V):
            mloc[p, 0, a] = tail[p][a]

    def backward_h(i, carry):
        c = cells - 1 - i
        new = []
        for p in range(2):
            u = rowsof(upp, c, p)
            pu = plus(matvec(u, carry[p][0]), [pres[c, p, a] for a in range(V)])
            qu = matvec(u, carry[p][1])
            for a in range(V):
                pres[c, p, a] = pu[a]
                qres[c, p, a] = qu[a]
            new.append([pu, qu])
        return new

    head = lax.fori_loop(0, cells, backward_h, [[[zero] * V, list(unit)] for _ in range(2)])
    for p in range(2):
        for a in range(V):
            mloc[p, 1, a] = head[p][1][a]
            mloc[p, 2, a] = head[p][0][a]
    mat_core = remote(mloc.at[1 - core], cmat.at[core], mcs, mcr, seg=mate)
    mat_core.start()

    @pl.loop(0, 3)
    def _(m):
        for a in range(V):
            cmat[core, m, a] = mloc[core, m, a]

    @pl.loop(0, cells)
    def _(c):
        for p in range(2):
            for a in range(V):
                inv[c, p, a] = inv16[c, p, a].astype(F32)

    remote(mloc.at[0], cmat.at[1 - core], mcs, mcr, seg=mate).wait_recv()

    def cm(c, m):
        return lambda a, k: cmat[c, m, a, pl.ds(k, 1), :]

    def cvals(c, m):
        return [cmat[c, m, a] for a in range(V)]

    chip_a = matvec(cm(1, 0), cvals(0, 0))
    chip_b = matvec(cm(0, 1), cvals(1, 1))
    chip_c = plus(matvec(cm(0, 1), matvec(cm(1, 2), cvals(0, 0))), cvals(0, 2))
    for m, mat in enumerate((chip_a, chip_b, chip_c)):
        for a in range(V):
            zmat[z, pl.ds(40 * m + a, V, stride=8), :] = mat[a][:V]

    def zm_copy(i, to):
        return remote(zmat.at[z], zmat.at[z], mzs.at[i], mzr.at[z], seg=to)

    @pl.loop(1, nz)
    def _(i):
        zm_copy(i, zpeer(i)[1]).start()

    wder[...] = split3(ewv[...] * rowv[pl.ds(2, 1), pl.ds(0, 1)])

    @pl.when(seg > 0)
    def _():
        ax_up.wait_recv()

    @pl.when(seg < nseg - 1)
    def _():
        ax_dn.wait_recv()

    @pl.loop(0, cells // 2)
    def _(h):
        for p in range(2):
            for v in range(V):
                timing = pair(wder, 2 * h, p, v)
                for j in range(2):
                    c = 2 * h + j
                    a1 = adv[c, p, pl.ds(v, 1), :]
                    v1 = vis[c, p, pl.ds(v, 1), :]
                    work[c, p, v] = (
                        a1 * (st[c, p, v] - st[c + 2, p, v])
                        + v1 * (st[c + 1, 1 - p, v] - 2.0 * st[c + 1, p, v])
                        - timing[j]
                    )

    def cols(ref, i, m):
        return [ref[i, pl.ds(40 * m + 8 * j, 8), :] for j in range(V)]

    def put(ref, i, m, mat):
        for j in range(V):
            ref[i, pl.ds(40 * m + 8 * j, 8), :] = mat[j]

    def z_responses():
        @pl.loop(1, nz)
        def _(i):
            zz, _s = zpeer(i)
            remote(zmat.at[zz], zmat.at[zz], mzs.at[i], mzr.at[zz], seg=mate).wait_recv()

        def ahead(d, s):
            put(resp, d, 0, s)
            return colmat(cols(zmat, d, 0), s)

        s_end = lax.fori_loop(0, nz, ahead, list(unit))

        def back(i, carry):
            d = nz - 1 - i
            pu, qu = carry
            put(resp, d, 1, pu)
            put(resp, d, 2, qu)
            b = cols(zmat, d, 1)
            return [plus(colmat(b, pu), colmat(cols(zmat, d, 2), cols(resp, d, 0))), colmat(b, qu)]

        pu, qu = lax.fori_loop(0, nz, back, [[zero] * V, list(unit)])
        put(xmat, x, 0, s_end)
        put(xmat, x, 1, qu)
        put(xmat, x, 2, pu)

        @pl.loop(1, nx)
        def _(i):
            remote(xmat.at[x], xmat.at[x], mxs.at[i], mxr.at[x], seg=xpeer(i)[1]).start()

    def x_responses():
        @pl.loop(1, nx)
        def _(i):
            xx, _s = xpeer(i)
            remote(xmat.at[xx], xmat.at[xx], mxs.at[i], mxr.at[xx], seg=mate).wait_recv()

    def tile_rows(k):
        t = lax.rem(k + tiles - 1, tiles)
        return pl.ds(pl.multiple_of(8 * t, 8), 8)

    def stage_local(k):
        at = tile_rows(k)
        for d in range(2):

            @pl.when(k == 0)
            def _():
                pitch_copy(0, d, True).wait_recv()

            @pl.when(k > 0)
            def _():
                src = state.at[:, 0, :, pl.ds(0, 8), :]
                remote(src, pit.at[d, :, :, pl.ds(0, 8), :], pits.at[d, k], pitr.at[d, k], pitch=yup).wait_recv()

        def ahead(c, carry):
            new = []
            for p in range(2):
                r = [work[c, p, v, at, :] + vis[c, p, pl.ds(v, 1), :] * pit[p, c, v, at, :] for v in range(V)]
                s = plus(matvec(rowsof(inv, c, p), r), matvec(rowsof(low, c, p), carry[p]))
                for a in range(V):
                    work[c, p, a, at, :] = s[a]
                new.append(s)
            return new

        ends = lax.fori_loop(0, cells, ahead, [[zero] * V for _ in range(2)])

        def back(i, carry):
            c = cells - 1 - i
            new = []
            for p in range(2):
                u = plus(matvec(rowsof(upp, c, p), carry[p]), [work[c, p, a, at, :] for a in range(V)])
                for a in range(V):
                    work[c, p, a, at, :] = u[a]
                new.append(u)
            return new

        heads = lax.fori_loop(0, cells, back, [[zero] * V for _ in range(2)])
        for p in range(2):
            for a in range(V):
                csend[k, p, a] = ends[p][a]
                csend[k, p, V + a] = heads[p][a]
        remote(csend.at[k, 1 - core], cbuf.at[k, core], cs.at[k], cr.at[k], seg=mate).start()
        for a in range(2 * V):
            cbuf[k, core, a] = csend[k, core, a]

    def stage_chip(k):
        remote(csend.at[k, 0], cbuf.at[k, 1 - core], cs.at[k], cr.at[k], seg=mate).wait_recv()
        b0, c0, b1, c1 = ([cbuf[k, c, o + a] for a in range(V)] for c in range(2) for o in (0, V))
        b = plus(matvec(cm(1, 0), b0), b1)
        c = plus(matvec(cm(0, 1), plus(matvec(cm(1, 2), b0), c1)), c0)
        for a in range(V):
            zsend[k, pl.ds(a, 8, stride=16), :] = b[a]
            zsend[k, pl.ds(8 + a, 8, stride=16), :] = c[a]

        @pl.loop(1, nz)
        def _(i):
            zz, to = zpeer(i)
            src = zsend.at[k, pl.ds(pl.multiple_of(16 * zz, 16), 16), :]
            remote(src, zbuf.at[k, z], zs.at[k, i], zr.at[k, z], seg=to).start()

        zbuf[k, z] = zsend[k, pl.ds(pl.multiple_of(16 * z, 16), 16), :]

    def half(ref, k, d, o):
        return ref[k, d, pl.ds(8 * o, 8), :]

    def stage_z(k):
        @pl.loop(1, nz)
        def _(i):
            zz, _s = zpeer(i)
            remote(zsend.at[k, pl.ds(0, 16), :], zbuf.at[k, zz], zs.at[k, i], zr.at[k, zz], seg=mate).wait_recv()

        def ahead(d, s):
            sol[k, d, pl.ds(0, 8), :] = s
            return colvec(cols(zmat, d, 0), s) + half(zbuf, k, d, 0)

        b = lax.fori_loop(0, nz, ahead, zero)

        def back(i, u):
            d = nz - 1 - i
            sol[k, d, pl.ds(8, 8), :] = u
            return (
                colvec(cols(zmat, d, 1), u) + colvec(cols(zmat, d, 2), half(sol, k, d, 0)) + half(zbuf, k, d, 1)
            )

        c = lax.fori_loop(0, nz, back, zero)
        xbuf[k, x, pl.ds(0, 8), :] = b
        xbuf[k, x, pl.ds(8, 8), :] = c

        @pl.loop(1, nx)
        def _(i):
            remote(xbuf.at[k, x], xbuf.at[k, x], xs.at[k, i], xr.at[k, x], seg=xpeer(i)[1]).start()

    def stage_x(k):
        @pl.loop(1, nx)
        def _(i):
            xx, _s = xpeer(i)
            remote(xbuf.at[k, xx], xbuf.at[k, xx], xs.at[k, i], xr.at[k, xx], seg=mate).wait_recv()

        def ahead(d, s):
            sx[d, pl.ds(0, 8), :] = s
            return colvec(cols(xmat, d, 0), s) + half(xbuf, k, d, 0)

        lax.fori_loop(0, nx, ahead, zero)

        def back(i, u):
            d = nx - 1 - i
            sx[d, pl.ds(8, 8), :] = u
            return (
                colvec(cols(xmat, d, 1), u)
                + colvec(cols(xmat, d, 2), sx[d, pl.ds(0, 8), :])
                + half(xbuf, k, d, 1)
            )

        lax.fori_loop(0, nx, back, zero)
        s_in, u_in = sx[x, pl.ds(0, 8), :], sx[x, pl.ds(8, 8), :]
        sb, ub = [bc(s_in, j) for j in range(V)], [bc(u_in, j) for j in range(V)]

        @pl.loop(0, nz)
        def _(d):
            ss, ps, qs = cols(resp, d, 0), cols(resp, d, 1), cols(resp, d, 2)
            ysend[k, d, pl.ds(0, 8), :] = half(sol, k, d, 0) + total([ss[j] * sb[j] for j in range(V)])
            ysend[k, d, pl.ds(8, 8), :] = half(sol, k, d, 1) + total(
                [ps[j] * sb[j] for j in range(V)] + [qs[j] * ub[j] for j in range(V)]
            )

        @pl.loop(1, nz)
        def _(i):
            zz, to = zpeer(i)
            dst = ybuf.at[k, pl.ds(pl.multiple_of(16 * z, 16), 16), :]
            remote(ysend.at[k, zz], dst, ys.at[k, i], yr.at[k, z], seg=to).start()

        ybuf[k, pl.ds(pl.multiple_of(16 * z, 16), 16), :] = ysend[k, z]

    def stage_back(k):
        @pl.loop(1, nz)
        def _(i):
            zz, _s = zpeer(i)
            dst = ybuf.at[k, pl.ds(pl.multiple_of(16 * zz, 16), 16), :]
            remote(ysend.at[k, 0], dst, ys.at[k, i], yr.at[k, zz], seg=mate).wait_recv()

        s0 = [ybuf[k, pl.ds(a, 8, stride=16), :] for a in range(V)]
        u1 = [ybuf[k, pl.ds(8 + a, 8, stride=16), :] for a in range(V)]
        s1 = plus(matvec(cm(0, 0), s0), [cbuf[k, 0, a] for a in range(V)])
        u0 = plus(plus(matvec(cm(1, 1), u1), matvec(cm(1, 2), s1)), [cbuf[k, 1, V + a] for a in range(V)])
        for c, (s, u) in enumerate(((s0, u0), (s1, u1))):
            for a in range(V):
                fsend[k, c, a] = s[a]
                fsend[k, c, V + a] = u[a]
        remote(fsend.at[k, 1 - core], infl.at[k, core], fs.at[k], fr.at[k], seg=mate).start()
        for a in range(2 * V):
            infl[k, core, a] = fsend[k, core, a]

    def out_copy(k, wait):
        at0 = pl.ds(8 * (tiles - 1), last)

        @pl.when(k == 0)
        def _():
            c = pltpu.make_async_copy(work.at[:, :, :, at0, :], out.at[:, :, :, at0, :], outs.at[k])
            c.wait() if wait else c.start()

        @pl.when(k > 0)
        def _():
            at = pl.ds(pl.multiple_of(8 * (jnp.maximum(k, 1) - 1), 8), 8)
            c = pltpu.make_async_copy(work.at[:, :, :, at, :], out.at[:, :, :, at, :], outs.at[k])
            c.wait() if wait else c.start()

    def stage_final(k):
        remote(fsend.at[k, 0], infl.at[k, 1 - core], fs.at[k], fr.at[k], seg=mate).wait_recv()
        at = tile_rows(k)
        s = [[infl[k, p, a] for a in range(V)] for p in range(2)]
        u = [[infl[k, p, V + a] for a in range(V)] for p in range(2)]

        @pl.loop(0, cells)
        def _(c):
            for p in range(2):
                fix = plus(matvec(rowsof(pres, c, p), s[p]), matvec(rowsof(qres, c, p), u[p]))
                for a in range(V):
                    work[c, p, a, at, :] = work[c, p, a, at, :] + fix[a]

        out_copy(k, False)

    @pl.loop(0, tiles + 4)
    def _(step):
        @pl.when(step < tiles)
        def _():
            stage_local(step)
            stage_chip(step)

        @pl.when(step == 1)
        def _():
            z_responses()

        @pl.when((step >= 1) & (step < tiles + 1))
        def _():
            stage_z(step - 1)

        @pl.when(step == 2)
        def _():
            x_responses()

        @pl.when((step >= 2) & (step < tiles + 2))
        def _():
            stage_x(step - 2)

        @pl.when((step >= 3) & (step < tiles + 3))
        def _():
            stage_back(step - 3)

        @pl.when(step >= 4)
        def _():
            stage_final(step - 4)

    @pl.when(seg < nseg - 1)
    def _():
        ax_up.wait_send()

    @pl.when(seg > 0)
    def _():
        ax_dn.wait_send()

    mat_core.wait_send()
    for d in range(2):
        for k in range(tiles):
            pitch_copy(k, d, True).wait_send()

    @pl.loop(1, nz)
    def _(i):
        zm_copy(i, mate).wait_send()

    @pl.loop(1, nx)
    def _(i):
        remote(xmat.at[x], xmat.at[x], mxs.at[i], mxr.at[x], seg=mate).wait_send()

    @pl.loop(0, tiles)
    def _(k):
        remote(csend.at[k, 0], cbuf.at[k, 0], cs.at[k], cr.at[k], seg=mate).wait_send()
        remote(fsend.at[k, 0], infl.at[k, 0], fs.at[k], fr.at[k], seg=mate).wait_send()

        @pl.loop(1, nz)
        def _(i):
            remote(zsend.at[k, pl.ds(0, 16), :], zbuf.at[k, 0], zs.at[k, i], zr.at[k, 0], seg=mate).wait_send()
            remote(ysend.at[k, 0], zbuf.at[k, 0], ys.at[k, i], yr.at[k, 0], seg=mate).wait_send()

        @pl.loop(1, nx)
        def _(i):
            remote(xbuf.at[k, 0], xbuf.at[k, 0], xs.at[k, i], xr.at[k, 0], seg=mate).wait_send()

        out_copy(k, True)


def local(nx, nz, ny, state, advect, viscous, inverse, lower, upper, blades, harmonic):
    cells, _, _, nt, _ = state.shape
    harm = harmonic.shape[0]
    ratio = blades[1].astype(F32) / blades[0].astype(F32)
    lag = 2.0 * math.pi * harmonic.astype(F32) * ratio
    angle = jnp.concatenate([jnp.zeros((1,), F32), lag, lag, jnp.zeros((R - 1 - 2 * harm,), F32)])
    row = jnp.stack([jnp.cos(angle), jnp.sin(angle), jnp.full((R,), ratio / harm)] + [jnp.zeros((R,), F32)] * 5)
    tiles = (nt + 7) // 8
    rows = 8 * tiles
    vm, dma = lambda *s: pltpu.VMEM(s, F32), lambda *s: pltpu.SemaphoreType.DMA(s)
    bf = lambda *s: pltpu.VMEM(s, jnp.bfloat16)
    scratch = [
        vm(cells + 2, 2, V, rows, R), vm(2, cells, V, rows, R), vm(cells, V, rows, R), vm(cells, 2, V, rows, R),
        vm(cells, 2, V, R), vm(cells, 2, V, R), bf(cells, 2, V, V, R), vm(cells, 2, V, V, R),
        vm(cells, 2, V, V, R), vm(cells, 2, V, V, R), vm(8, R), vm(rows, R), vm(rows, R), vm(R, 2 * R), vm(rows, 2 * R),
        bf(rows, 3 * PACK), bf(rows, 3 * PACK),
        vm(cells, 2, V, 8, R), vm(cells, 2, V, 8, R), vm(2, 3, V, 8, R), vm(2, 3, V, 8, R),
        vm(nz, 120, R), vm(nz, 120, R), vm(nx, 120, R),
        vm(tiles, 2, 2 * V, 8, R), vm(tiles, 2, 2 * V, 8, R), vm(tiles, 16 * nz, R), vm(tiles, nz, 16, R),
        vm(tiles, nz, 16, R), vm(tiles, nx, 16, R), vm(nx, 16, R), vm(tiles, nz, 16, R), vm(tiles, 16 * nz, R),
        vm(tiles, 2, 2 * V, 8, R), vm(tiles, 2, 2 * V, 8, R),
        dma(11), dma(2), dma(2), dma(2, tiles), dma(2, tiles), pltpu.SemaphoreType.DMA, pltpu.SemaphoreType.DMA,
        dma(nz), dma(nz), dma(nx), dma(nx),
        dma(tiles), dma(tiles), dma(tiles, nz), dma(tiles, nz), dma(tiles, nx), dma(tiles, nx),
        dma(tiles, nz), dma(tiles, nz), dma(tiles), dma(tiles), dma(tiles),
    ]
    return pl.pallas_call(
        functools.partial(kernel, nx, nz, ny, cells, nt),
        out_shape=jax.ShapeDtypeStruct(state.shape, F32),
        in_specs=[ANY] * 11,
        out_specs=ANY,
        scratch_shapes=scratch,
        compiler_params=pltpu.CompilerParams(collective_id=0, has_side_effects=True),
        name="line_update",
    )(state, advect, viscous, inverse, lower, upper, row, *tables(nt))


def solution(mesh):
    nz = 8
    nx, ny = mesh.shape["seg"] // (2 * nz), mesh.shape["pitch"]
    five, four = P("seg", "pitch", None, None, None), P("seg", "pitch", None, None)
    return jax.shard_map(
        functools.partial(local, nx, nz, ny),
        mesh=mesh,
        in_specs=(five, four, four, five, five, five, P(), P()),
        out_specs=five,
        check_vma=False,
    )
```

```python
import functools
import math

import jax
import jax.numpy as jnp
import numpy as np
from jax import lax
from jax.experimental import pallas as pl
from jax.experimental.pallas import tpu as pltpu
from jax.sharding import PartitionSpec as P

MESH = pl.DeviceIdType.MESH
ANY = pl.BlockSpec(memory_space=pl.ANY)
V = 5
R = 128
PACK = 64
F32 = jnp.float32


def tables(nt):
    harm = (nt - 1) // 2
    n = np.arange(nt)
    diff = n[:, None] - n[None, :]
    derive = np.where(diff == 0, 0.0, 0.5 * (1 - 2 * (diff % 2)) / np.where(diff == 0, 1.0, np.sin(np.pi * diff / nt)))
    angle = 2 * np.pi * ((n[:, None] * np.arange(1, harm + 1)[None, :]) % nt) / nt
    cosine, sine = np.cos(angle), np.sin(angle)
    rows = 56
    x = np.zeros((rows, R))
    y = np.zeros((rows, R))
    x[:nt, 0] = 1.0 / nt
    x[:nt, 1 : harm + 1], x[:nt, harm + 1 : nt] = 2 * cosine / nt, 2 * sine / nt
    y[:nt, 1 : harm + 1], y[:nt, harm + 1 : nt] = -2 * sine / nt, 2 * cosine / nt
    right = np.zeros((R, 2 * R))
    wide = np.zeros((rows, 2 * R))
    for third in range(3):
        at = slice(third * PACK, third * PACK + nt)
        right[0, at] = 1.0
        right[1 : harm + 1, at], right[harm + 1 : nt, at] = cosine.T, sine.T
        wide[:nt, at] = derive
    return tuple(np.asarray(a, np.float32) for a in (x, y, right, wide))


def bc(tile, k):
    return jnp.broadcast_to(tile[k : k + 1, :], (8, R))


def total(terms):
    terms = list(terms)
    while len(terms) > 1:
        terms = [a + b for a, b in zip(terms[::2], terms[1::2])] + ([terms[-1]] if len(terms) % 2 else [])
    return terms[0]


def matvec(row, vec):
    return [total([row(a, k) * vec[k] for k in range(V)]) for a in range(V)]


def colvec(cols, vec):
    return total([cols[k] * bc(vec, k) for k in range(V)])


def colmat(cols, mat):
    return [colvec(cols, m) for m in mat]


def plus(a, b):
    return [x + y for x, y in zip(a, b)]


def kernel(
    nx, nz, ny, cells, nt,
    state, advect, viscous, inverse, lower, upper, blades, harmonic, ex, ey, eright, ewide,
    out,
    st, pit, ghost, work, adv, vis, inv16, inv, low, upp, exv, eyv, erv, ewv, wder, wghost,
    pres, qres, mloc, cmat, zmat, resp, xmat,
    csend, cbuf, zsend, zbuf, sol, xbuf, sx, ysend, ybuf, fsend, infl,
    ld, axs, axr, pits, pitr, mcs, mcr, mzs, mzr, mxs, mxr,
    cs, cr, zs, zr, xs, xr, ys, yr, fs, fr, outs,
):
    tiles = (nt + 7) // 8
    last = nt - 8 * (tiles - 1)
    seg = lax.axis_index("seg")
    y = lax.axis_index("pitch")
    core = lax.rem(seg, 2)
    z = lax.rem(seg // 2, nz)
    x = seg // (2 * nz)
    nseg = 2 * nx * nz
    mate = seg + 1 - 2 * core
    yup, ydn = lax.rem(y + 1, ny), lax.rem(y + ny - 1, ny)

    def zpeer(i):
        zz = lax.rem(z + i, nz)
        return zz, (x * nz + zz) * 2 + core

    def xpeer(i):
        xx = lax.rem(x + i, nx)
        return xx, (xx * nz + z) * 2 + core

    def remote(src, dst, send, recv, **to):
        return pltpu.make_async_remote_copy(
            src_ref=src, dst_ref=dst, send_sem=send, recv_sem=recv, device_id=to, device_id_type=MESH
        )

    @pl.loop(0, cells + 2)
    def _(c):
        for p in range(2):
            for v in range(V):
                st[c, p, v, pl.ds(nt, 8 * tiles - nt), :] = jnp.zeros((8 * tiles - nt, R), F32)

    loads = [
        pltpu.make_async_copy(ex, exv, ld.at[0]),
        pltpu.make_async_copy(ey, eyv, ld.at[1]),
        pltpu.make_async_copy(eright, erv, ld.at[2]),
        pltpu.make_async_copy(ewide, ewv, ld.at[3]),
    ]
    for p in range(2):
        dst = st.at[pl.ds(1, cells), p, :, pl.ds(0, nt), :]
        loads.append(pltpu.make_async_copy(state.at[:, :, :, p, :], dst, ld.at[4 + p]))
    for j, (src, dst) in enumerate(((lower, low), (upper, upp))):
        for p in range(2):
            loads.append(pltpu.make_async_copy(src.at[:, :, :, p, :], dst.at[:, p], ld.at[6 + 2 * j + p]))
    for j, (src, dst) in enumerate(((advect, adv), (viscous, vis))):
        for p in range(2):
            loads.append(pltpu.make_async_copy(src.at[:, :, p, :], dst.at[:, p], ld.at[10 + 2 * j + p]))
    loads.append(pltpu.make_async_copy(inverse, inv16, ld.at[14]))
    for c in loads:
        c.start()

    barrier = pltpu.get_barrier_semaphore()

    def greet(**to):
        pl.semaphore_signal(barrier, inc=1, device_id=to, device_id_type=MESH)

    greet(pitch=yup)
    greet(pitch=ydn)
    greet(seg=mate)
    greet(seg=lax.rem(seg + 1, nseg))
    greet(seg=lax.rem(seg + nseg - 1, nseg))

    @pl.loop(1, nz)
    def _(i):
        greet(seg=zpeer(i)[1])

    @pl.loop(1, nx)
    def _(i):
        greet(seg=xpeer(i)[1])

    pl.semaphore_wait(barrier, 5 + nz - 1 + nx - 1)

    def rows_of(k):
        return pl.ds(8 * (tiles - 1), last) if k == 0 else pl.ds(8 * (k - 1), 8)

    def pitch_copy(k, d, raw, cellrange=None):
        at = rows_of(k)
        zr_ = pl.ds(0, cells) if cellrange is None else cellrange
        src = state.at[zr_, :, at, 1 - d, :] if raw else ghost.at[zr_, :, at, :]
        return remote(
            src, pit.at[d, zr_, :, at, :], pits.at[d, k], pitr.at[d, k], pitch=yup if d == 0 else ydn
        )

    for d in range(2):
        wraps = (y == ny - 1) if d == 0 else (y == 0)

        @pl.when(jnp.logical_not(wraps))
        def _():
            for k in range(tiles):
                pitch_copy(k, d, True).start()

    def axial(j, p):
        cell, slot, to = ((cells - 1, 0, seg + 1), (0, cells + 1, seg + nseg - 1))[j]
        dst = st.at[slot, p, :, pl.ds(0, nt), :]
        return remote(state.at[cell, :, :, p, :], dst, axs.at[j, p], axr.at[j, p], seg=lax.rem(to, nseg))

    def has_axial(j, receive):
        return seg > 0 if (j == 0) == receive else seg < nseg - 1

    for j in range(2):

        @pl.when(has_axial(j, False))
        def _():
            for p in range(2):
                axial(j, p).start()

    for edge, cell in ((seg == 0, 0), (seg == nseg - 1, cells + 1)):

        @pl.when(edge)
        def _():
            for p in range(2):
                for v in range(V):
                    st[cell, p, v, pl.ds(0, nt), :] = jnp.zeros((nt, R), F32)

    rotor, stator = blades[0].astype(F32), blades[1].astype(F32)

    def split3(wide):
        high = wide.astype(jnp.bfloat16)
        low_ = (wide - high.astype(F32)).astype(jnp.bfloat16)
        lane = lax.broadcasted_iota(jnp.int32, wide.shape, 1)
        return jnp.where(lane < 2 * PACK, high.astype(F32), low_.astype(F32)).astype(jnp.bfloat16)[:, : 3 * PACK]

    def stacked(cell):
        s = jnp.concatenate([cell, jnp.zeros((PACK - 8 * tiles, R), F32)], 0)
        high = s.astype(jnp.bfloat16)
        low_ = (s - high.astype(F32)).astype(jnp.bfloat16)
        return jnp.concatenate([high, low_, high], 0)

    def pair(weights, c, p, v):
        rhs = jnp.concatenate([stacked(st[1 + c, p, v]), stacked(st[2 + c, p, v])], 1)
        both = jnp.dot(weights[...], rhs, preferred_element_type=F32)
        return both[:, :R], both[:, R:]

    for c in loads[:6]:
        c.wait()

    @pl.when((y == 0) | (y == ny - 1))
    def _():
        sign = jnp.where(y == 0, 1.0, -1.0).astype(F32)
        lane = lax.broadcasted_iota(jnp.int32, (8, R), 1)
        mode = jnp.zeros((8, R), F32)
        for k in range((nt - 1) // 2):
            hit = (lane == 1 + k) | (lane == 1 + k + (nt - 1) // 2)
            mode = jnp.where(hit, harmonic[k].astype(F32), mode)
        turns = mode * stator / rotor
        angle = (2.0 * math.pi) * (turns - jnp.floor(turns + 0.5))
        e = exv[...] * jnp.cos(angle)[:1] + eyv[...] * (jnp.sin(angle)[:1] * sign)
        wghost[...] = split3(jnp.dot(e, erv[...], precision=lax.Precision.HIGHEST, preferred_element_type=F32))
        p = jnp.where(y == 0, 0, 1)

        @pl.loop(0, cells // 2)
        def _(h):
            for v in range(V):
                a, b = pair(wghost, 2 * h, p, v)
                ghost[2 * h, v] = a
                ghost[2 * h + 1, v] = b
            for d in range(2):

                @pl.when((y == ny - 1) if d == 0 else (y == 0))
                def _():
                    for k in range(2):
                        pitch_copy(k, d, False, pl.ds(2 * h, 2)).start()

        for d in range(2):

            @pl.when((y == ny - 1) if d == 0 else (y == 0))
            def _():
                for k in range(2, tiles):
                    pitch_copy(k, d, False).start()

    for c in loads[6:]:
        c.wait()

    sub = lax.broadcasted_iota(jnp.int32, (8, R), 0)
    unit = [jnp.where(sub == v, 1.0, 0.0).astype(F32) for v in range(V)]
    zero = jnp.zeros((8, R), F32)

    def rowsof(ref, c, p):
        return lambda a, k: ref[c, p, a, pl.ds(k, 1), :]

    def forward_h(c, carry):
        new = []
        for p in range(2):
            h = matvec(rowsof(low, c, p), carry[p])
            for a in range(V):
                pres[c, p, a] = h[a]
            new.append(h)
        return new

    tail = lax.fori_loop(0, cells, forward_h, [list(unit), list(unit)])
    for p in range(2):
        for a in range(V):
            mloc[p, 0, a] = tail[p][a]

    def backward_h(i, carry):
        c = cells - 1 - i
        new = []
        for p in range(2):
            u = rowsof(upp, c, p)
            pu = plus(matvec(u, carry[p][0]), [pres[c, p, a] for a in range(V)])
            qu = matvec(u, carry[p][1])
            for a in range(V):
                pres[c, p, a] = pu[a]
                qres[c, p, a] = qu[a]
            new.append([pu, qu])
        return new

    head = lax.fori_loop(0, cells, backward_h, [[[zero] * V, list(unit)] for _ in range(2)])
    for p in range(2):
        for a in range(V):
            mloc[p, 1, a] = head[p][1][a]
            mloc[p, 2, a] = head[p][0][a]
    mat_core = remote(mloc.at[1 - core], cmat.at[core], mcs, mcr, seg=mate)
    mat_core.start()

    @pl.loop(0, 3)
    def _(m):
        for a in range(V):
            cmat[core, m, a] = mloc[core, m, a]

    @pl.loop(0, cells)
    def _(c):
        for a in range(V):
            for k in range(V):
                both = inv16[c, a, k].astype(F32)
                for p in range(2):
                    inv[c, p, a, pl.ds(k, 1), :] = both[p : p + 1]

    remote(mloc.at[0], cmat.at[1 - core], mcs, mcr, seg=mate).wait_recv()

    def cm(c, m):
        return lambda a, k: cmat[c, m, a, pl.ds(k, 1), :]

    def cvals(c, m):
        return [cmat[c, m, a] for a in range(V)]

    chip_a = matvec(cm(1, 0), cvals(0, 0))
    chip_b = matvec(cm(0, 1), cvals(1, 1))
    chip_c = plus(matvec(cm(0, 1), matvec(cm(1, 2), cvals(0, 0))), cvals(0, 2))
    for m, mat in enumerate((chip_a, chip_b, chip_c)):
        for a in range(V):
            zmat[z, pl.ds(40 * m + a, V, stride=8), :] = mat[a][:V]

    def zm_copy(i, to):
        return remote(zmat.at[z], zmat.at[z], mzs.at[i], mzr.at[z], seg=to)

    @pl.loop(1, nz)
    def _(i):
        zm_copy(i, zpeer(i)[1]).start()

    wder[...] = split3(ewv[...] * (jnp.full((1, 2 * R), stator, F32) / jnp.full((1, 2 * R), rotor * ((nt - 1) // 2), F32)))

    for j in range(2):

        @pl.when(has_axial(j, True))
        def _():
            for p in range(2):
                axial(j, p).wait_recv()

    @pl.loop(0, cells // 2)
    def _(h):
        for p in range(2):
            for v in range(V):
                timing = pair(wder, 2 * h, p, v)
                for j in range(2):
                    c = 2 * h + j
                    a1 = adv[c, p, pl.ds(v, 1), :]
                    v1 = vis[c, p, pl.ds(v, 1), :]
                    work[c, p, v] = (
                        a1 * (st[c, p, v] - st[c + 2, p, v])
                        + v1 * (st[c + 1, 1 - p, v] - 2.0 * st[c + 1, p, v])
                        - timing[j]
                    )

    def cols(ref, i, m):
        return [ref[i, pl.ds(40 * m + 8 * j, 8), :] for j in range(V)]

    def put(ref, i, m, mat):
        for j in range(V):
            ref[i, pl.ds(40 * m + 8 * j, 8), :] = mat[j]

    def z_responses():
        @pl.loop(1, nz)
        def _(i):
            zz, _s = zpeer(i)
            remote(zmat.at[zz], zmat.at[zz], mzs.at[i], mzr.at[zz], seg=mate).wait_recv()

        def ahead(d, s):
            put(resp, d, 0, s)
            return colmat(cols(zmat, d, 0), s)

        s_end = lax.fori_loop(0, nz, ahead, list(unit))

        def back(i, carry):
            d = nz - 1 - i
            pu, qu = carry
            put(resp, d, 1, pu)
            put(resp, d, 2, qu)
            b = cols(zmat, d, 1)
            return [plus(colmat(b, pu), colmat(cols(zmat, d, 2), cols(resp, d, 0))), colmat(b, qu)]

        pu, qu = lax.fori_loop(0, nz, back, [[zero] * V, list(unit)])
        put(xmat, x, 0, s_end)
        put(xmat, x, 1, qu)
        put(xmat, x, 2, pu)

        @pl.loop(1, nx)
        def _(i):
            remote(xmat.at[x], xmat.at[x], mxs.at[i], mxr.at[x], seg=xpeer(i)[1]).start()

    def x_responses():
        @pl.loop(1, nx)
        def _(i):
            xx, _s = xpeer(i)
            remote(xmat.at[xx], xmat.at[xx], mxs.at[i], mxr.at[xx], seg=mate).wait_recv()

    def tile_rows(k):
        t = lax.rem(k + tiles - 1, tiles)
        return pl.ds(pl.multiple_of(8 * t, 8), 8)

    def stage_local(k):
        at = tile_rows(k)
        for d in range(2):

            @pl.when(k == 0)
            def _():
                pitch_copy(0, d, True).wait_recv()

            @pl.when(k > 0)
            def _():
                src = state.at[:, :, pl.ds(0, 8), 0, :]
                remote(src, pit.at[d, :, :, pl.ds(0, 8), :], pits.at[d, k], pitr.at[d, k], pitch=yup).wait_recv()

        def ahead(c, carry):
            new = []
            for p in range(2):
                r = [work[c, p, v, at, :] + vis[c, p, pl.ds(v, 1), :] * pit[p, c, v, at, :] for v in range(V)]
                s = plus(matvec(rowsof(inv, c, p), r), matvec(rowsof(low, c, p), carry[p]))
                for a in range(V):
                    work[c, p, a, at, :] = s[a]
                new.append(s)
            return new

        ends = lax.fori_loop(0, cells, ahead, [[zero] * V for _ in range(2)])

        def back(i, carry):
            c = cells - 1 - i
            new = []
            for p in range(2):
                u = plus(matvec(rowsof(upp, c, p), carry[p]), [work[c, p, a, at, :] for a in range(V)])
                for a in range(V):
                    work[c, p, a, at, :] = u[a]
                new.append(u)
            return new

        heads = lax.fori_loop(0, cells, back, [[zero] * V for _ in range(2)])
        for p in range(2):
            for a in range(V):
                csend[k, p, a] = ends[p][a]
                csend[k, p, V + a] = heads[p][a]
        remote(csend.at[k, 1 - core], cbuf.at[k, core], cs.at[k], cr.at[k], seg=mate).start()
        for a in range(2 * V):
            cbuf[k, core, a] = csend[k, core, a]

    def stage_chip(k):
        remote(csend.at[k, 0], cbuf.at[k, 1 - core], cs.at[k], cr.at[k], seg=mate).wait_recv()
        b0, c0, b1, c1 = ([cbuf[k, c, o + a] for a in range(V)] for c in range(2) for o in (0, V))
        b = plus(matvec(cm(1, 0), b0), b1)
        c = plus(matvec(cm(0, 1), plus(matvec(cm(1, 2), b0), c1)), c0)
        for a in range(V):
            zsend[k, pl.ds(a, 8, stride=16), :] = b[a]
            zsend[k, pl.ds(8 + a, 8, stride=16), :] = c[a]

        @pl.loop(1, nz)
        def _(i):
            zz, to = zpeer(i)
            src = zsend.at[k, pl.ds(pl.multiple_of(16 * zz, 16), 16), :]
            remote(src, zbuf.at[k, z], zs.at[k, i], zr.at[k, z], seg=to).start()

        zbuf[k, z] = zsend[k, pl.ds(pl.multiple_of(16 * z, 16), 16), :]

    def half(ref, k, d, o):
        return ref[k, d, pl.ds(8 * o, 8), :]

    def stage_z(k):
        @pl.loop(1, nz)
        def _(i):
            zz, _s = zpeer(i)
            remote(zsend.at[k, pl.ds(0, 16), :], zbuf.at[k, zz], zs.at[k, i], zr.at[k, zz], seg=mate).wait_recv()

        def ahead(d, s):
            sol[k, d, pl.ds(0, 8), :] = s
            return colvec(cols(zmat, d, 0), s) + half(zbuf, k, d, 0)

        b = lax.fori_loop(0, nz, ahead, zero)

        def back(i, u):
            d = nz - 1 - i
            sol[k, d, pl.ds(8, 8), :] = u
            return (
                colvec(cols(zmat, d, 1), u) + colvec(cols(zmat, d, 2), half(sol, k, d, 0)) + half(zbuf, k, d, 1)
            )

        c = lax.fori_loop(0, nz, back, zero)
        xbuf[k, x, pl.ds(0, 8), :] = b
        xbuf[k, x, pl.ds(8, 8), :] = c

        @pl.loop(1, nx)
        def _(i):
            remote(xbuf.at[k, x], xbuf.at[k, x], xs.at[k, i], xr.at[k, x], seg=xpeer(i)[1]).start()

    def stage_x(k):
        @pl.loop(1, nx)
        def _(i):
            xx, _s = xpeer(i)
            remote(xbuf.at[k, xx], xbuf.at[k, xx], xs.at[k, i], xr.at[k, xx], seg=mate).wait_recv()

        def ahead(d, s):
            sx[d, pl.ds(0, 8), :] = s
            return colvec(cols(xmat, d, 0), s) + half(xbuf, k, d, 0)

        lax.fori_loop(0, nx, ahead, zero)

        def back(i, u):
            d = nx - 1 - i
            sx[d, pl.ds(8, 8), :] = u
            return (
                colvec(cols(xmat, d, 1), u)
                + colvec(cols(xmat, d, 2), sx[d, pl.ds(0, 8), :])
                + half(xbuf, k, d, 1)
            )

        lax.fori_loop(0, nx, back, zero)
        s_in, u_in = sx[x, pl.ds(0, 8), :], sx[x, pl.ds(8, 8), :]
        sb, ub = [bc(s_in, j) for j in range(V)], [bc(u_in, j) for j in range(V)]

        @pl.loop(0, nz)
        def _(d):
            ss, ps, qs = cols(resp, d, 0), cols(resp, d, 1), cols(resp, d, 2)
            ysend[k, d, pl.ds(0, 8), :] = half(sol, k, d, 0) + total([ss[j] * sb[j] for j in range(V)])
            ysend[k, d, pl.ds(8, 8), :] = half(sol, k, d, 1) + total(
                [ps[j] * sb[j] for j in range(V)] + [qs[j] * ub[j] for j in range(V)]
            )

        @pl.loop(1, nz)
        def _(i):
            zz, to = zpeer(i)
            dst = ybuf.at[k, pl.ds(pl.multiple_of(16 * z, 16), 16), :]
            remote(ysend.at[k, zz], dst, ys.at[k, i], yr.at[k, z], seg=to).start()

        ybuf[k, pl.ds(pl.multiple_of(16 * z, 16), 16), :] = ysend[k, z]

    def stage_back(k):
        @pl.loop(1, nz)
        def _(i):
            zz, _s = zpeer(i)
            dst = ybuf.at[k, pl.ds(pl.multiple_of(16 * zz, 16), 16), :]
            remote(ysend.at[k, 0], dst, ys.at[k, i], yr.at[k, zz], seg=mate).wait_recv()

        s0 = [ybuf[k, pl.ds(a, 8, stride=16), :] for a in range(V)]
        u1 = [ybuf[k, pl.ds(8 + a, 8, stride=16), :] for a in range(V)]
        s1 = plus(matvec(cm(0, 0), s0), [cbuf[k, 0, a] for a in range(V)])
        u0 = plus(plus(matvec(cm(1, 1), u1), matvec(cm(1, 2), s1)), [cbuf[k, 1, V + a] for a in range(V)])
        for c, (s, u) in enumerate(((s0, u0), (s1, u1))):
            for a in range(V):
                fsend[k, c, a] = s[a]
                fsend[k, c, V + a] = u[a]
        remote(fsend.at[k, 1 - core], infl.at[k, core], fs.at[k], fr.at[k], seg=mate).start()
        for a in range(2 * V):
            infl[k, core, a] = fsend[k, core, a]

    def out_copy(k, wait):
        at0 = pl.ds(8 * (tiles - 1), last)

        def both(at):
            for p in range(2):
                c = pltpu.make_async_copy(work.at[:, p, :, at, :], out.at[:, :, at, p, :], outs.at[k, p])
                c.wait() if wait else c.start()

        @pl.when(k == 0)
        def _():
            both(at0)

        @pl.when(k > 0)
        def _():
            both(pl.ds(pl.multiple_of(8 * (jnp.maximum(k, 1) - 1), 8), 8))

    def stage_final(k):
        remote(fsend.at[k, 0], infl.at[k, 1 - core], fs.at[k], fr.at[k], seg=mate).wait_recv()
        at = tile_rows(k)
        s = [[infl[k, p, a] for a in range(V)] for p in range(2)]
        u = [[infl[k, p, V + a] for a in range(V)] for p in range(2)]

        @pl.loop(0, cells)
        def _(c):
            for p in range(2):
                fix = plus(matvec(rowsof(pres, c, p), s[p]), matvec(rowsof(qres, c, p), u[p]))
                for a in range(V):
                    work[c, p, a, at, :] = work[c, p, a, at, :] + fix[a]

        out_copy(k, False)

    @pl.loop(0, tiles + 4)
    def _(step):
        @pl.when(step < tiles)
        def _():
            stage_local(step)
            stage_chip(step)

        @pl.when(step == 1)
        def _():
            z_responses()

        @pl.when((step >= 1) & (step < tiles + 1))
        def _():
            stage_z(step - 1)

        @pl.when(step == 2)
        def _():
            x_responses()

        @pl.when((step >= 2) & (step < tiles + 2))
        def _():
            stage_x(step - 2)

        @pl.when((step >= 3) & (step < tiles + 3))
        def _():
            stage_back(step - 3)

        @pl.when(step >= 4)
        def _():
            stage_final(step - 4)

    for j in range(2):

        @pl.when(has_axial(j, False))
        def _():
            for p in range(2):
                axial(j, p).wait_send()

    mat_core.wait_send()
    for d in range(2):
        for k in range(tiles):
            pitch_copy(k, d, True).wait_send()

    @pl.loop(1, nz)
    def _(i):
        zm_copy(i, mate).wait_send()

    @pl.loop(1, nx)
    def _(i):
        remote(xmat.at[x], xmat.at[x], mxs.at[i], mxr.at[x], seg=mate).wait_send()

    @pl.loop(0, tiles)
    def _(k):
        remote(csend.at[k, 0], cbuf.at[k, 0], cs.at[k], cr.at[k], seg=mate).wait_send()
        remote(fsend.at[k, 0], infl.at[k, 0], fs.at[k], fr.at[k], seg=mate).wait_send()

        @pl.loop(1, nz)
        def _(i):
            remote(zsend.at[k, pl.ds(0, 16), :], zbuf.at[k, 0], zs.at[k, i], zr.at[k, 0], seg=mate).wait_send()
            remote(ysend.at[k, 0], zbuf.at[k, 0], ys.at[k, i], yr.at[k, 0], seg=mate).wait_send()

        @pl.loop(1, nx)
        def _(i):
            remote(xbuf.at[k, 0], xbuf.at[k, 0], xs.at[k, i], xr.at[k, 0], seg=mate).wait_send()

        out_copy(k, True)


def local(nx, nz, ny, state, advect, viscous, inverse, lower, upper, blades, harmonic):
    cells, _, _, nt, _ = state.shape
    tiles = (nt + 7) // 8
    rows = 8 * tiles
    vm, dma = lambda *s: pltpu.VMEM(s, F32), lambda *s: pltpu.SemaphoreType.DMA(s)
    bf = lambda *s: pltpu.VMEM(s, jnp.bfloat16)
    scratch = [
        vm(cells + 2, 2, V, rows, R), vm(2, cells, V, rows, R), vm(cells, V, rows, R), vm(cells, 2, V, rows, R),
        vm(cells, 2, V, R), vm(cells, 2, V, R), bf(cells, V, V, 2, R), vm(cells, 2, V, V, R),
        vm(cells, 2, V, V, R), vm(cells, 2, V, V, R), vm(rows, R), vm(rows, R), vm(R, 2 * R), vm(rows, 2 * R),
        bf(rows, 3 * PACK), bf(rows, 3 * PACK),
        vm(cells, 2, V, 8, R), vm(cells, 2, V, 8, R), vm(2, 3, V, 8, R), vm(2, 3, V, 8, R),
        vm(nz, 120, R), vm(nz, 120, R), vm(nx, 120, R),
        vm(tiles, 2, 2 * V, 8, R), vm(tiles, 2, 2 * V, 8, R), vm(tiles, 16 * nz, R), vm(tiles, nz, 16, R),
        vm(tiles, nz, 16, R), vm(tiles, nx, 16, R), vm(nx, 16, R), vm(tiles, nz, 16, R), vm(tiles, 16 * nz, R),
        vm(tiles, 2, 2 * V, 8, R), vm(tiles, 2, 2 * V, 8, R),
        dma(15), dma(2, 2), dma(2, 2), dma(2, tiles), dma(2, tiles), pltpu.SemaphoreType.DMA, pltpu.SemaphoreType.DMA,
        dma(nz), dma(nz), dma(nx), dma(nx),
        dma(tiles), dma(tiles), dma(tiles, nz), dma(tiles, nz), dma(tiles, nx), dma(tiles, nx),
        dma(tiles, nz), dma(tiles, nz), dma(tiles), dma(tiles), dma(tiles, 2),
    ]
    smem = pl.BlockSpec(memory_space=pltpu.SMEM)
    out = pl.pallas_call(
        functools.partial(kernel, nx, nz, ny, cells, nt),
        out_shape=jax.ShapeDtypeStruct((cells, V, nt, 2, R), F32),
        in_specs=[ANY] * 6 + [smem] * 2 + [ANY] * 4,
        out_specs=ANY,
        scratch_shapes=scratch,
        compiler_params=pltpu.CompilerParams(collective_id=0, has_side_effects=True),
        name="line_update",
    )(
        *(jnp.moveaxis(a, 1, -2) for a in (state, advect, viscous, inverse, lower, upper)),
        blades, harmonic, *tables(nt),
    )
    return jnp.moveaxis(out, -2, 1)


def solution(mesh):
    nz = 8
    nx, ny = mesh.shape["seg"] // (2 * nz), mesh.shape["pitch"]
    five, four = P("seg", "pitch", None, None, None), P("seg", "pitch", None, None)
    return jax.shard_map(
        functools.partial(local, nx, nz, ny),
        mesh=mesh,
        in_specs=(five, four, four, five, five, five, P(), P()),
        out_specs=five,
        check_vma=False,
    )
```
